128 devices in a mesh: grp: 8 (over x, z_hi), fac: 16 (over y, z_lo, core).
Axes of the slice: x: 4, y: 4, z: 4 (z_hi: 2, z_lo: 2; z = z_hi * 2 + z_lo), core: 2. Of those that a mesh axis runs over, the one named last changes fastest.
Arguments:
- metric_panels: bfloat16 [32768, 2048], P('fac'), may hold values from -0.1875 to 0.1875
- diag_inverses: float32 [2, 1024, 1024], replicated, as said below
- pair_batch: bfloat16 [32768, 8192], P('fac', 'grp'), may hold values from -6 to 6
Outputs:
- solved: bfloat16 [32768, 8192], P('fac', 'grp')
The draws below stay inside these ranges and needn't reach their ends.
Inputs may be any that keep to these rules, and one draw needn't show every extreme that they name: `diag_inverses`: each of the two blocks is lower triangular with a positive diagonal.
All inputs are finite; a program needn't handle non-finite values.
Results may differ from the reference program's by a relative error of at most 0.006.
Values may be sent and summed in bfloat16 or wider, within the bound.
No kernel may reach another device: no remote copies, remote signals or barrier semaphores. Data moves between devices by JAX's collectives and lax.ppermute only.
A program may use at most 128 MiB of HBM per device.

```python
import jax
import jax.numpy as jnp
from jax import lax

PANEL = 1024
AUXROWS = 32768
PAIRS = 8192


def draw_diag_inverses(key, part):
    key_diag, key_low = jax.random.split(jax.random.fold_in(key, 7141))
    diagonal = jnp.exp(jax.random.uniform(key_diag, (2, PANEL), jnp.float32, jnp.log(0.6), jnp.log(1.6)))
    spread = 0.45 / jnp.sqrt(jnp.float32(PANEL))
    lower = jax.random.normal(key_low, (2, PANEL, PANEL), jnp.float32) * spread
    row_index = jnp.arange(PANEL)[:, None]
    col_index = jnp.arange(PANEL)[None, :]
    strict = (col_index < row_index).astype(jnp.float32)
    identity = (col_index == row_index).astype(jnp.float32)
    return lower * strict[None] + diagonal[:, :, None] * identity[None]


def block_levels(rng, dims, pieces, least, largest):
    gain, own = 1.0, jax.random.fold_in(rng, 6)
    for axis_at, shards_of in pieces:
        heights = jnp.exp(jax.random.uniform(jax.random.fold_in(own, axis_at), (shards_of,), jnp.float32, least / len(pieces), largest / len(pieces)))
        gain = gain * jnp.repeat(heights, dims[axis_at] // shards_of).reshape([-1 if axis == axis_at else 1 for axis in range(len(dims))])
    return gain


def scatter_about(key, extent, scale, most, cuts=(), dtype=jnp.bfloat16):
    loudness = block_levels(key, extent, cuts, -0.22, 0.18) if cuts else 1.0
    values = jax.random.normal(key, extent, jnp.float32) * scale * loudness
    return jnp.minimum(jnp.maximum(values, -most), most).astype(dtype)


def setup_inputs(seed: int = 0) -> dict:
    splits = jax.random.split(jax.random.key(seed), 4)
    metric_panels = scatter_about(splits[0], (AUXROWS, 2 * PANEL), PANEL ** -0.5, 0.1875, ((0, 16),))
    diag_inverses = draw_diag_inverses(jax.random.fold_in(splits[3], 71), 0)
    pair_batch = scatter_about(splits[2], (AUXROWS, PAIRS), 1.0, 6.0, ((0, 16), (1, 8)))
    return {"metric_panels": metric_panels, "diag_inverses": diag_inverses, "pair_batch": pair_batch}


def reference(metric_panels, diag_inverses, pair_batch):
    highest = lax.Precision.HIGHEST
    first_inverse = diag_inverses[0]
    second_inverse = diag_inverses[1]
    metric_float = metric_panels.astype(jnp.float32)
    factor_first = jnp.dot(metric_float[:, :PANEL], first_inverse.T, precision=highest, preferred_element_type=jnp.float32)
    cross = factor_first[PANEL:2 * PANEL]
    updated = metric_float[:, PANEL:2 * PANEL] - jnp.dot(factor_first, cross.T, precision=highest, preferred_element_type=jnp.float32)
    factor_second = jnp.dot(updated, second_inverse.T, precision=highest, preferred_element_type=jnp.float32)
    batch_float = pair_batch.astype(jnp.float32)
    first = jnp.dot(first_inverse, batch_float[:PANEL], precision=highest, preferred_element_type=jnp.float32)
    corrected = batch_float[PANEL:2 * PANEL] - jnp.dot(cross, first, precision=highest, preferred_element_type=jnp.float32)
    second = jnp.dot(second_inverse, corrected, precision=highest, preferred_element_type=jnp.float32)
    rest = batch_float[2 * PANEL:] - jnp.dot(factor_first[2 * PANEL:], first, precision=highest, preferred_element_type=jnp.float32)
    rest = rest - jnp.dot(factor_second[2 * PANEL:], second, precision=highest, preferred_element_type=jnp.float32)
    return jnp.concatenate([first, second, rest], axis=0).astype(jnp.bfloat16)
```

```python
import jax
import jax.numpy as jnp
from jax import lax
from jax.sharding import PartitionSpec as P


def dot(left, right, left_dim=1, right_dim=0):
    return lax.dot_general(
        left,
        right,
        (((left_dim,), (right_dim,)), ((), ())),
        preferred_element_type=jnp.float32,
    )


def split_inverse(inverse):
    rounded = lax.reduce_precision(inverse, 8, 7)
    low = jnp.diagonal(inverse) - jnp.diagonal(rounded)
    return rounded.astype(jnp.bfloat16), low


def owner_chain(metric_panels, diag_inverses, pair_batch):
    size = diag_inverses.shape[1]
    half = jnp.bfloat16
    w0, d0 = split_inverse(diag_inverses[0])
    w1, d1 = split_inverse(diag_inverses[1])
    panel = metric_panels[size : 2 * size, :size]
    upper, lower = pair_batch[:size], pair_batch[size : 2 * size]
    cross = (dot(panel, w0, 1, 1) + panel.astype(jnp.float32) * d0[None, :]).astype(half)
    first = dot(w0, upper) + d0[:, None] * upper.astype(jnp.float32)
    corrected = lower.astype(jnp.float32) - dot(cross, first.astype(half))
    second = dot(w1, corrected.astype(half)) + d1[:, None] * corrected
    y_second = (dot(w1, second.astype(half), 0, 0) + d1[:, None] * second).astype(half)
    inner = first - dot(cross, y_second, 0, 0)
    y_first = (dot(w0, inner.astype(half), 0, 0) + d0[:, None] * inner).astype(half)
    solved = jnp.concatenate([first.astype(half), second.astype(half)], axis=0)
    return solved, y_first, y_second


def body(metric_panels, diag_inverses, pair_batch):
    size = diag_inverses.shape[1]
    members = lax.axis_size("fac")
    chips = members // 2
    rows = size // chips
    fac = lax.axis_index("fac")
    core = lax.rem(fac, 2)
    chip = lax.div(fac, 2)

    solved, y_first, y_second = owner_chain(metric_panels, diag_inverses, pair_batch)
    handed = lax.ppermute(y_second, "fac", [(0, 1)])
    carried = jnp.where(core == 0, y_first, handed)
    own = jnp.where(chip == 0, carried[:rows], jnp.zeros_like(carried[:rows]))
    for target in range(1, chips):
        piece = carried[rows * target : rows * (target + 1)]
        own = own + lax.ppermute(
            piece, "fac", [(0, 2 * target), (1, 2 * target + 1)]
        )
    groups = [[2 * c + k for c in range(chips)] for k in range(2)]
    spread = jnp.broadcast_to(own[None], (chips,) + own.shape).reshape(size, own.shape[1])
    full = lax.all_to_all(spread, "fac", 0, 0, axis_index_groups=groups, tiled=True)
    other = lax.ppermute(full, "fac", [(i, i ^ 1) for i in range(members)])
    metric_own = lax.dynamic_slice_in_dim(metric_panels, core * size, size, 1)
    metric_other = lax.dynamic_slice_in_dim(metric_panels, (1 - core) * size, size, 1)
    rest = pair_batch.astype(jnp.float32) - dot(metric_own, full)
    rest = rest - dot(metric_other, other)
    return jnp.where(fac == 0, solved, rest.astype(jnp.bfloat16))


def solution(mesh):
    in_specs = (P("fac", None), P(), P("fac", "grp"))
    out_specs = P("fac", "grp")
    return jax.shard_map(body, mesh=mesh, in_specs=in_specs, out_specs=out_specs, check_vma=False)
```
